256 devices in a mesh: depth: 16 (over x, y), tile: 16 (over z, core).
Axes of the slice: x: 4, y: 4, z: 8, core: 2. Of those that a mesh axis runs over, the one named last changes fastest.
Arguments:
- density: float32 [512, 512, 2048], P('depth', 'tile'), may hold values from 0 to 1
- palette: float32 [2, 3], replicated, may hold values from 0.2 to 1
- light_dir: float32 [2, 3], replicated, may hold values from -4 to 4
- slab_of: int32 [16], replicated, may hold values from 0 to 15, each once
Outputs:
- images: float32 [2, 4, 512, 2048], P(None, None, 'tile', 'depth')
The draws below stay inside these ranges and needn't reach their ends.
Inputs may be any that keep to these rules, and one draw needn't show every extreme that they name: `slab_of`: each of 0 to 15 appears once.
All inputs are finite; a program needn't handle non-finite values.
Results may differ from the reference program's by a relative error of at most 0.0008.
Values may be sent and summed in bfloat16 or wider, within the bound.
No kernel may reach another device: no remote copies, remote signals or barrier semaphores. Data moves between devices by JAX's collectives and lax.ppermute only.
A program may use at most 128 MiB of HBM per device.

```python
import jax
import jax.numpy as jnp
from jax import lax

CZ = 32
NX = 512
NY = 2048
NZ = 512
N_DEPTH = 16


def level_of(rng, shape, pieces, least, largest):
    factor_of, own = 1.0, jax.random.fold_in(rng, 6)
    for axis_at, shards_of in pieces:
        heights = jnp.exp(jax.random.uniform(jax.random.fold_in(own, axis_at), (shards_of,), jnp.float32, least / len(pieces), largest / len(pieces)))
        factor_of = factor_of * jnp.repeat(heights, shape[axis_at] // shards_of).reshape([-1 if axis == axis_at else 1 for axis in range(len(shape))])
    return factor_of


def scatter_about(own_key, shape, deviation, bound, kind=jnp.bfloat16):
    values = jax.random.normal(own_key, shape, jnp.float32) * deviation
    return jnp.minimum(jnp.maximum(values, -bound), bound).astype(kind)


def setup_inputs(seed: int = 0) -> dict:
    streams_of = jax.random.split(jax.random.key(seed), 5)
    density = jnp.clip(1.0 * jax.random.uniform(streams_of[0], (NZ, NX, NY), jnp.float32) ** level_of(streams_of[0], (NZ, NX, NY), ((0, 16), (1, 16)), -0.2, 0.2), 0.0, 1.0)
    palette = jnp.clip(jax.random.uniform(streams_of[1], (2, 3), jnp.float32, 0.2, 1.0), 0.2, 1.0)
    light_dir = scatter_about(streams_of[2], (2, 3), 1.0, 4.0, jnp.float32)
    slab_of = jax.random.permutation(streams_of[3], N_DEPTH).astype(jnp.int32)
    return dict(density=density, palette=palette, light_dir=light_dir, slab_of=slab_of)


HIGH = lax.Precision.HIGHEST

def centred(field, axis):
    size = field.shape[axis]
    upper = jnp.concatenate([lax.slice_in_dim(field, 1, size, axis=axis), lax.slice_in_dim(field, size - 1, size, axis=axis)], axis)
    lower = jnp.concatenate([lax.slice_in_dim(field, 0, 1, axis=axis), lax.slice_in_dim(field, 0, size - 1, axis=axis)], axis)
    return (upper - lower) * 0.5

def march(block, grad_x, palette, light_dir, factor):
    grad_z = centred(block, 0)
    grad_y = centred(block, 2)
    length = jnp.sqrt(grad_x * grad_x + grad_y * grad_y + grad_z * grad_z + 0.25)
    optical = block * factor
    opacity = 1.0 - jnp.exp(-optical)
    running = jnp.cumsum(optical, axis=0)
    slab_tau = running[-1]
    before = [running - optical, slab_tau[None] - running]
    colours = []
    for view in range(2):
        facing = grad_x * light_dir[view, 0] + grad_y * light_dir[view, 1] + grad_z * light_dir[view, 2]
        shade = 0.3 + jnp.abs(facing) / length
        weight = opacity * jnp.exp(-before[view]) * shade
        plain = lax.optimization_barrier(jnp.sum(weight, axis=0))
        dense = lax.optimization_barrier(jnp.sum(block * weight, axis=0))
        colours.append(palette[0][:, None, None] * plain[None] + palette[1][:, None, None] * dense[None])
    return (jnp.stack(colours).astype(jnp.bfloat16), slab_tau.astype(jnp.bfloat16))

def compose(slab_rgb, slab_tau, slab_of):
    tau_full = slab_tau.astype(jnp.float32)
    earlier = (slab_of[None, :] < slab_of[:, None]).astype(jnp.float32)
    later = (slab_of[None, :] > slab_of[:, None]).astype(jnp.float32)
    front_one = jnp.einsum('jk,kxy->jxy', earlier, tau_full, precision=HIGH)
    front_two = jnp.einsum('jk,kxy->jxy', later, tau_full, precision=HIGH)
    rgb_full = slab_rgb.astype(jnp.float32)
    colour_one = jnp.einsum('jcxy,jxy->cxy', rgb_full[:, 0], jnp.exp(-front_one), precision=HIGH)
    colour_two = jnp.einsum('jcxy,jxy->cxy', rgb_full[:, 1], jnp.exp(-front_two), precision=HIGH)
    coverage = 1.0 - jnp.exp(-lax.optimization_barrier(jnp.sum(tau_full, axis=0)))
    return jnp.stack([jnp.concatenate([colour_one, coverage[None]], 0), jnp.concatenate([colour_two, coverage[None]], 0)])

def reference(density, palette, light_dir, slab_of):
    factor = 3.0 / NZ

    def one_block(index):
        block = lax.dynamic_slice_in_dim(density, index * CZ, CZ, 0)
        return march(block, centred(block, 1), palette, light_dir, factor)
    slab_rgb, slab_tau = lax.map(one_block, jnp.arange(N_DEPTH, dtype=jnp.int32))
    return compose(slab_rgb, slab_tau, slab_of)
```

```python
import functools
import math

import jax
import jax.numpy as jnp
from jax import lax
from jax.experimental import pallas as pl
from jax.experimental.pallas import tpu as pltpu
from jax.sharding import PartitionSpec as P

LANES = 128
GROUP = 8
CHANNELS = 7
MIB = 2**20
LOG2E = math.log2(math.e)


def march(centre, differences, z_rows, light, factor):
    value = centre(0)
    below = value
    zero = jnp.zeros(value.shape, jnp.float32)
    plain_0 = dense_0 = plain_1 = dense_1 = total = zero
    passed = jnp.ones(value.shape, jnp.float32)
    for z in range(z_rows):
        above = centre(z + 1) if z + 1 < z_rows else value
        diff_x, diff_y = differences(z, value)
        diff_z = above - below
        inverse = lax.rsqrt(diff_x * diff_x + diff_y * diff_y + diff_z * diff_z + 1.0)
        fade = jnp.exp2(value * (-factor * LOG2E))
        opacity = 1.0 - fade
        shade_0, shade_1 = (
            0.3 + jnp.abs(diff_x * a + diff_y * b + diff_z * c) * inverse for a, b, c in light
        )
        weight_0 = passed * opacity * shade_0
        weight_1 = opacity * shade_1
        plain_0 = plain_0 + weight_0
        dense_0 = dense_0 + value * weight_0
        plain_1 = plain_1 * fade + weight_1
        dense_1 = dense_1 * fade + value * weight_1
        passed = passed * fade
        total = total + value
        below, value = value, above
    return plain_0, dense_0, plain_1, dense_1, total * factor


def write_pixels(out, c, start, sums, palette):
    plain_0, dense_0, plain_1, dense_1, tau = sums
    rows = pl.ds(start, tau.shape[0])
    for view, (plain, dense) in enumerate(((plain_0, dense_0), (plain_1, dense_1))):
        for k in range(3):
            colour = palette[0][k] * plain + palette[1][k] * dense
            out[c, view * 3 + k, rows, :] = colour.astype(jnp.bfloat16)
    out[c, 6, rows, :] = tau.astype(jnp.bfloat16)


def y_difference(buf, c, z, rows, value, first, last):
    left = buf[c, z, rows, :]
    right = buf[c + 2, z, rows, :]
    following = pltpu.roll(jnp.where(first, right, value), LANES - 1, 1)
    preceding = pltpu.roll(jnp.where(last, left, value), 1, 1)
    return following - preceding


def march_kernel(factor, outer, *refs):
    if outer:
        density, low, high, palette_ref, light_ref, place_ref = refs[:6]
        out, buf, sems = refs[6:]
    else:
        density, palette_hbm, light_hbm = refs[:3]
        out, low_out, high_out, buf, sems, palette_ref, light_ref, small = refs[3:]
    z_rows, x_rows, columns = density.shape
    count = columns // LANES

    def fetch(c):
        lanes = pl.ds(pl.multiple_of(c * LANES, LANES), LANES)
        return pltpu.make_async_copy(density.at[:, :, lanes], buf.at[c + 1], sems.at[c])

    for c in range(count):
        fetch(c).start()
    if not outer:
        pltpu.make_async_copy(palette_hbm, palette_ref, small.at[0]).start()
        pltpu.make_async_copy(light_hbm, light_ref, small.at[1]).start()
        pltpu.make_async_copy(palette_hbm, palette_ref, small.at[0]).wait()
        pltpu.make_async_copy(light_hbm, light_ref, small.at[1]).wait()
    shape = (2 * GROUP, LANES)
    lane = lax.broadcasted_iota(jnp.int32, shape, 1)
    first, last = lane == 0, lane == LANES - 1
    light = [[light_ref[v, k] for k in range(3)] for v in range(2)]
    palette = [[palette_ref[i, k] for k in range(3)] for i in range(2)]
    fetch(0).wait()
    buf[0] = pltpu.roll(buf[1], LANES - 1, 2)

    def body(c, carry):
        @pl.when(c + 1 < count)
        def _():
            fetch(c + 1).wait()

        @pl.when(c + 1 == count)
        def _():
            buf[count + 1] = pltpu.roll(buf[count], 1, 2)

        lanes = pl.ds(pl.multiple_of(c * LANES, LANES), LANES)
        if outer:
            tile = place_ref[0]
            row = lax.broadcasted_iota(jnp.int32, (GROUP, LANES), 0)
            is_low, is_high = row == 0, row == GROUP - 1
            own_low = jnp.full((GROUP, LANES), tile, jnp.int32) == 0
            own_high = jnp.full((GROUP, LANES), tile, jnp.int32) == place_ref[1] - 1
            top = x_rows - GROUP

            def centre(z):
                return jnp.concatenate([buf[c + 1, z, :GROUP, :], buf[c + 1, z, top:, :]], 0)

            def differences(z, value):
                head, tail = value[:GROUP], value[GROUP:]
                lo = jnp.where(own_low, head, low[z : z + 1, lanes])
                hi = jnp.where(own_high, tail, high[z : z + 1, lanes])
                head_x = buf[c + 1, z, 1 : GROUP + 1, :] - jnp.where(
                    is_low, lo, pltpu.roll(head, 1, 0)
                )
                tail_x = (
                    jnp.where(is_high, hi, pltpu.roll(tail, GROUP - 1, 0))
                    - buf[c + 1, z, top - 1 : x_rows - 1, :]
                )
                left = jnp.concatenate([buf[c, z, :GROUP, :], buf[c, z, top:, :]], 0)
                right = jnp.concatenate([buf[c + 2, z, :GROUP, :], buf[c + 2, z, top:, :]], 0)
                following = pltpu.roll(jnp.where(first, right, value), LANES - 1, 1)
                preceding = pltpu.roll(jnp.where(last, left, value), 1, 1)
                return jnp.concatenate([head_x, tail_x], 0), following - preceding

            sums = march(centre, differences, z_rows, light, factor)
            write_pixels(out, c, 0, sums, palette)
        else:
            for z in range(z_rows):
                low_out[z : z + 1, lanes] = buf[c + 1, z, 0:1, :]
                high_out[z : z + 1, lanes] = buf[c + 1, z, x_rows - 1 : x_rows, :]
            for start in range(GROUP, x_rows - GROUP, 2 * GROUP):
                rows = pl.ds(start, 2 * GROUP)

                def centre(z, rows=rows):
                    return buf[c + 1, z, rows, :]

                def differences(z, value, start=start, rows=rows):
                    diff_x = (
                        buf[c + 1, z, pl.ds(start + 1, 2 * GROUP), :]
                        - buf[c + 1, z, pl.ds(start - 1, 2 * GROUP), :]
                    )
                    return diff_x, y_difference(buf, c, z, rows, value, first, last)

                sums = march(centre, differences, z_rows, light, factor)
                write_pixels(out, c, start - GROUP, sums, palette)
        return carry

    lax.fori_loop(0, count, body, 0)


def march_inner(density, palette, light_dir, factor):
    z_rows, x_rows, columns = density.shape
    count = columns // LANES
    hbm = pl.BlockSpec(memory_space=pltpu.HBM)
    vmem = pl.BlockSpec(memory_space=pltpu.VMEM)
    plane = jax.ShapeDtypeStruct((z_rows, columns), jnp.float32)
    return pl.pallas_call(
        functools.partial(march_kernel, factor, False),
        out_shape=(
            jax.ShapeDtypeStruct((count, CHANNELS, x_rows - 2 * GROUP, LANES), jnp.bfloat16),
            plane,
            plane,
        ),
        in_specs=[hbm, hbm, hbm],
        out_specs=(vmem, vmem, vmem),
        scratch_shapes=[
            pltpu.VMEM((count + 2, z_rows, x_rows, LANES), jnp.float32),
            pltpu.SemaphoreType.DMA((count,)),
            pltpu.SMEM((2, 3), jnp.float32),
            pltpu.SMEM((2, 3), jnp.float32),
            pltpu.SemaphoreType.DMA((2,)),
        ],
        compiler_params=pltpu.CompilerParams(vmem_limit_bytes=57 * MIB),
        name="march_inner",
    )(density, palette, light_dir)


def march_outer(density, low, high, palette, light_dir, place, factor):
    z_rows, x_rows, columns = density.shape
    count = columns // LANES
    smem = pl.BlockSpec(memory_space=pltpu.SMEM)
    vmem = pl.BlockSpec(memory_space=pltpu.VMEM)
    return pl.pallas_call(
        functools.partial(march_kernel, factor, True),
        out_shape=jax.ShapeDtypeStruct((count, CHANNELS, 2 * GROUP, LANES), jnp.bfloat16),
        in_specs=[pl.BlockSpec(memory_space=pltpu.HBM), vmem, vmem, smem, smem, smem],
        out_specs=vmem,
        scratch_shapes=[
            pltpu.VMEM((count + 2, z_rows, x_rows, LANES), jnp.float32),
            pltpu.SemaphoreType.DMA((count,)),
        ],
        compiler_params=pltpu.CompilerParams(vmem_limit_bytes=57 * MIB),
        name="march_outer",
    )(density, low, high, palette, light_dir, place)


def compose_kernel(slab_ref, inner, outer, out, order):
    slabs, _, inner_rows, lanes = inner.shape
    for b in range(slabs):
        order[slab_ref[b]] = b
    for source, pieces in (
        (inner, ((0, inner_rows, GROUP),)),
        (outer, ((0, GROUP, 0), (GROUP, GROUP, GROUP + inner_rows))),
    ):
        shape = source.shape[2:]
        images = []
        for view in range(2):
            front = jnp.zeros(shape, jnp.float32)
            colours = [jnp.zeros(shape, jnp.float32) for _ in range(3)]
            for position in range(slabs) if view == 0 else reversed(range(slabs)):
                b = order[position]
                fading = jnp.exp(-front)
                for k in range(3):
                    colours[k] += source[b, view * 3 + k].astype(jnp.float32) * fading
                front = front + source[b, 6].astype(jnp.float32)
            images.append(colours + [1.0 - jnp.exp(-front)])
        for view in range(2):
            for k in range(4):
                image = images[0][3] if k == 3 else images[view][k]
                for start, size, target in pieces:
                    out[view, k, target : target + size, :] = image[start : start + size]


def compose(slab_of, inner, outer):
    vmem = pl.BlockSpec(memory_space=pltpu.VMEM)
    rows = inner.shape[2] + outer.shape[2]
    return pl.pallas_call(
        compose_kernel,
        out_shape=jax.ShapeDtypeStruct((2, 4, rows, LANES), jnp.float32),
        in_specs=[pl.BlockSpec(memory_space=pltpu.SMEM), vmem, vmem],
        out_specs=vmem,
        scratch_shapes=[pltpu.SMEM((slab_of.shape[0],), jnp.int32)],
        compiler_params=pltpu.CompilerParams(vmem_limit_bytes=8 * MIB),
        name="compose",
    )(slab_of, inner, outer)


def on_device(density, palette, light_dir, slab_of):
    factor = 3.0 / (density.shape[0] * lax.axis_size("depth"))
    tiles = lax.axis_size("tile")
    forward = [(i, i + 1) for i in range(tiles - 1)]
    backward = [(i + 1, i) for i in range(tiles - 1)]
    inner, low, high = march_inner(density, palette, light_dir, factor)
    from_low = lax.ppermute(high, "tile", forward)
    from_high = lax.ppermute(low, "tile", backward)
    inner_all = lax.all_to_all(inner, "depth", 0, 0, tiled=True)
    place = jnp.stack([lax.axis_index("tile"), jnp.int32(tiles)])
    outer = march_outer(density, from_low, from_high, palette, light_dir, place, factor)
    outer_all = lax.all_to_all(outer, "depth", 0, 0, tiled=True)
    return compose(slab_of, inner_all, outer_all)


def solution(mesh):
    in_specs = (P("depth", "tile", None), P(), P(), P())
    out_specs = P(None, None, "tile", "depth")
    return jax.shard_map(
        on_device, mesh=mesh, in_specs=in_specs, out_specs=out_specs, check_vma=False
    )
```

```python
import functools
import math

import jax
import jax.numpy as jnp
from jax import lax
from jax.experimental import pallas as pl
from jax.experimental.pallas import tpu as pltpu
from jax.sharding import PartitionSpec as P

LANES = 128
GROUP = 8
CHANNELS = 7
MIB = 2**20
LOG2E = math.log2(math.e)


def march(centre, differences, z_rows, light, factor):
    value = centre(0)
    below = value
    plain_0 = dense_0 = plain_1 = dense_1 = total = jnp.zeros(value.shape, jnp.float32)
    passed = grown = jnp.ones(value.shape, jnp.float32)
    for z in range(z_rows):
        above = centre(z + 1) if z + 1 < z_rows else value
        diff_x, diff_y = differences(z, value)
        diff_z = above - below
        inverse = lax.rsqrt(diff_x * diff_x + diff_y * diff_y + diff_z * diff_z + 1.0)
        shade_0, shade_1 = (
            0.3 + jnp.abs(diff_x * a + diff_y * b + diff_z * c) * inverse for a, b, c in light
        )
        total = total + value
        passed_next = jnp.exp2(total * (-factor * LOG2E))
        grown_next = jnp.exp2(total * (factor * LOG2E))
        weight_0 = (passed - passed_next) * shade_0
        weight_1 = (grown_next - grown) * shade_1
        plain_0 = plain_0 + weight_0
        dense_0 = dense_0 + value * weight_0
        plain_1 = plain_1 + weight_1
        dense_1 = dense_1 + value * weight_1
        passed, grown = passed_next, grown_next
        below, value = value, above
    return plain_0, dense_0, plain_1 * passed, dense_1 * passed, total * factor


def write_pixels(out, c, start, sums, palette):
    plain_0, dense_0, plain_1, dense_1, tau = sums
    rows = pl.ds(start, tau.shape[0])
    for view, (plain, dense) in enumerate(((plain_0, dense_0), (plain_1, dense_1))):
        for k in range(3):
            colour = palette[0][k] * plain + palette[1][k] * dense
            out[c, view * 3 + k, rows, :] = colour.astype(jnp.bfloat16)
    out[c, 6, rows, :] = tau.astype(jnp.bfloat16)


def y_difference(buf, c, z, rows, value, first, last):
    left = buf[c, z, rows, :]
    right = buf[c + 2, z, rows, :]
    following = pltpu.roll(jnp.where(first, right, value), LANES - 1, 1)
    preceding = pltpu.roll(jnp.where(last, left, value), 1, 1)
    return following - preceding


def planes_kernel(density, low, high, sems):
    x_rows = density.shape[1]
    copies = [
        pltpu.make_async_copy(density.at[:, x, :], target, sems.at[i])
        for i, (x, target) in enumerate(((0, low), (x_rows - 1, high)))
    ]
    for copy in copies:
        copy.start()
    for copy in copies:
        copy.wait()


def boundary_planes(density):
    z_rows, _, columns = density.shape
    plane = jax.ShapeDtypeStruct((z_rows, columns), jnp.float32)
    vmem = pl.BlockSpec(memory_space=pltpu.VMEM)
    return pl.pallas_call(
        planes_kernel,
        out_shape=(plane, plane),
        in_specs=[pl.BlockSpec(memory_space=pltpu.HBM)],
        out_specs=(vmem, vmem),
        scratch_shapes=[pltpu.SemaphoreType.DMA((2,))],
        compiler_params=pltpu.CompilerParams(vmem_limit_bytes=2 * MIB),
        name="planes",
    )(density)


def scalars_of(ref, rows, columns):
    return [[ref[i, k] for k in range(columns)] for i in range(rows)]


def lane_edges(shape):
    lane = lax.broadcasted_iota(jnp.int32, shape, 1)
    return lane == 0, lane == LANES - 1


def inner_kernel(factor, density, palette_hbm, light_hbm, out, field, sems, palette_ref, light_ref, small):
    z_rows, x_rows, columns = density.shape
    count = columns // LANES

    def fetch(c):
        lanes = pl.ds(pl.multiple_of(c * LANES, LANES), LANES)
        return pltpu.make_async_copy(density.at[:, :, lanes], field.at[c + 1], sems.at[c])

    scalars = [
        pltpu.make_async_copy(palette_hbm, palette_ref, small.at[0]),
        pltpu.make_async_copy(light_hbm, light_ref, small.at[1]),
    ]
    for copy in scalars:
        copy.start()
    for c in range(count):
        fetch(c).start()
    for copy in scalars:
        copy.wait()
    first, last = lane_edges((2 * GROUP, LANES))
    light = scalars_of(light_ref, 2, 3)
    palette = scalars_of(palette_ref, 2, 3)
    fetch(0).wait()
    field[0] = pltpu.roll(field[1], LANES - 1, 2)

    def body(c, carry):
        @pl.when(c + 1 < count)
        def _():
            fetch(c + 1).wait()

        @pl.when(c + 1 == count)
        def _():
            field[count + 1] = pltpu.roll(field[count], 1, 2)

        for start in range(GROUP, x_rows - GROUP, 2 * GROUP):
            rows = pl.ds(start, 2 * GROUP)

            def centre(z, rows=rows):
                return field[c + 1, z, rows, :]

            def differences(z, value, start=start, rows=rows):
                diff_x = (
                    field[c + 1, z, pl.ds(start + 1, 2 * GROUP), :]
                    - field[c + 1, z, pl.ds(start - 1, 2 * GROUP), :]
                )
                return diff_x, y_difference(field, c, z, rows, value, first, last)

            write_pixels(out, c, start, march(centre, differences, z_rows, light, factor), palette)
        return carry

    lax.fori_loop(0, count, body, 0)


def march_inner(density, palette, light_dir, factor):
    z_rows, x_rows, columns = density.shape
    count = columns // LANES
    hbm = pl.BlockSpec(memory_space=pltpu.HBM)
    vmem = pl.BlockSpec(memory_space=pltpu.VMEM)
    return pl.pallas_call(
        functools.partial(inner_kernel, factor),
        out_shape=(
            jax.ShapeDtypeStruct((count, CHANNELS, x_rows, LANES), jnp.bfloat16),
            pltpu.VMEM((count + 2, z_rows, x_rows, LANES), jnp.float32),
        ),
        in_specs=[hbm, hbm, hbm],
        out_specs=(vmem, vmem),
        scratch_shapes=[
            pltpu.SemaphoreType.DMA((count,)),
            pltpu.SMEM((2, 3), jnp.float32),
            pltpu.SMEM((2, 3), jnp.float32),
            pltpu.SemaphoreType.DMA((2,)),
        ],
        compiler_params=pltpu.CompilerParams(vmem_limit_bytes=4 * MIB),
        name="march_inner",
    )(density, palette, light_dir)


def outer_kernel(factor, tiles, field, low, high, palette_ref, light_ref, tile_ref, _, out):
    count, z_rows, x_rows = field.shape[0] - 2, field.shape[1], field.shape[2]
    top = x_rows - GROUP
    first, last = lane_edges((2 * GROUP, LANES))
    light = scalars_of(light_ref, 2, 3)
    palette = scalars_of(palette_ref, 2, 3)
    row = lax.broadcasted_iota(jnp.int32, (GROUP, LANES), 0)
    is_low, is_high = row == 0, row == GROUP - 1
    tile = jnp.full((GROUP, LANES), tile_ref[0], jnp.int32)
    own_low, own_high = tile == 0, tile == tiles - 1

    def body(c, carry):
        lanes = pl.ds(pl.multiple_of(c * LANES, LANES), LANES)

        def both(block, z):
            return jnp.concatenate([field[block, z, :GROUP, :], field[block, z, top:, :]], 0)

        def centre(z):
            return both(c + 1, z)

        def differences(z, value):
            head, tail = value[:GROUP], value[GROUP:]
            before = jnp.where(own_low, head, low[z : z + 1, lanes])
            after = jnp.where(own_high, tail, high[z : z + 1, lanes])
            before = jnp.where(is_low, before, pltpu.roll(head, 1, 0))
            after = jnp.where(is_high, after, pltpu.roll(tail, GROUP - 1, 0))
            diff_x = jnp.concatenate(
                [
                    field[c + 1, z, 1 : GROUP + 1, :] - before,
                    after - field[c + 1, z, top - 1 : x_rows - 1, :],
                ],
                0,
            )
            following = pltpu.roll(jnp.where(first, both(c + 2, z), value), LANES - 1, 1)
            preceding = pltpu.roll(jnp.where(last, both(c, z), value), 1, 1)
            return diff_x, following - preceding

        sums = march(centre, differences, z_rows, light, factor)
        write_pixels(out, c, 0, [s[:GROUP] for s in sums], palette)
        write_pixels(out, c, top, [s[GROUP:] for s in sums], palette)
        return carry

    lax.fori_loop(0, count, body, 0)


def march_outer(field, low, high, palette, light_dir, tile, tiles, colours, factor):
    smem = pl.BlockSpec(memory_space=pltpu.SMEM)
    vmem = pl.BlockSpec(memory_space=pltpu.VMEM)
    return pl.pallas_call(
        functools.partial(outer_kernel, factor, tiles),
        out_shape=jax.ShapeDtypeStruct(colours.shape, jnp.bfloat16),
        in_specs=[vmem, vmem, vmem, smem, smem, smem, vmem],
        out_specs=vmem,
        input_output_aliases={6: 0},
        compiler_params=pltpu.CompilerParams(vmem_limit_bytes=4 * MIB),
        name="march_outer",
    )(field, low, high, palette, light_dir, tile, colours)


def compose_kernel(slab_ref, source, out, order):
    slabs = source.shape[0]
    for b in range(slabs):
        order[slab_ref[b]] = b
    shape = source.shape[2:]
    for view in range(2):
        front = jnp.zeros(shape, jnp.float32)
        colours = [jnp.zeros(shape, jnp.float32) for _ in range(3)]
        for position in range(slabs) if view == 0 else reversed(range(slabs)):
            b = order[position]
            fading = jnp.exp(-front)
            for k in range(3):
                colours[k] += source[b, view * 3 + k].astype(jnp.float32) * fading
            front = front + source[b, 6].astype(jnp.float32)
        for k in range(3):
            out[view, k] = colours[k]
        if view == 0:
            out[0, 3] = out[1, 3] = 1.0 - jnp.exp(-front)


def compose(slab_of, source):
    vmem = pl.BlockSpec(memory_space=pltpu.VMEM)
    return pl.pallas_call(
        compose_kernel,
        out_shape=jax.ShapeDtypeStruct((2, 4, *source.shape[2:]), jnp.float32),
        in_specs=[pl.BlockSpec(memory_space=pltpu.SMEM), vmem],
        out_specs=vmem,
        scratch_shapes=[pltpu.SMEM((slab_of.shape[0],), jnp.int32)],
        compiler_params=pltpu.CompilerParams(vmem_limit_bytes=4 * MIB),
        name="compose",
    )(slab_of, source)


def on_device(density, palette, light_dir, slab_of):
    factor = 3.0 / (density.shape[0] * lax.axis_size("depth"))
    tiles = lax.axis_size("tile")
    forward = [(i, i + 1) for i in range(tiles - 1)]
    backward = [(i + 1, i) for i in range(tiles - 1)]
    density, palette_hbm, light_hbm = (
        pltpu.with_memory_space_constraint(a, pltpu.HBM) for a in (density, palette, light_dir)
    )
    low, high = boundary_planes(density)
    from_low = lax.ppermute(high, "tile", forward)
    from_high = lax.ppermute(low, "tile", backward)
    colours, field = march_inner(density, palette_hbm, light_hbm, factor)
    tile = lax.axis_index("tile")[None]
    colours = march_outer(
        field, from_low, from_high, palette, light_dir, tile, tiles, colours, factor
    )
    return compose(slab_of, lax.all_to_all(colours, "depth", 0, 0, tiled=True))


def solution(mesh):
    in_specs = (P("depth", "tile", None), P(), P(), P())
    out_specs = P(None, None, "tile", "depth")
    return jax.shard_map(
        on_device, mesh=mesh, in_specs=in_specs, out_specs=out_specs, check_vma=False
    )
```

```python
import functools
import math

import jax
import jax.numpy as jnp
from jax import lax
from jax.experimental import pallas as pl
from jax.experimental.pallas import tpu as pltpu
from jax.sharding import PartitionSpec as P

LANES = 128
GROUP = 8
CHANNELS = 5
AMBIENT = 0.3
MIB = 2**20
UNROLL = 4
OUTER = 16
LOG2E = math.log2(math.e)


def march(centre, differences, z_rows, light, adder, factor):
    value = centre(0)
    below = value
    total = jnp.zeros(value.shape, jnp.float32)
    passed = grown = jnp.ones(value.shape, jnp.float32)
    depth = adder.shape[1] // value.shape[0]
    sums = [jnp.zeros((value.shape[0], 2 * LANES), jnp.float32) for _ in range(2)]
    terms = [([], []), ([], [])]
    for z in range(z_rows):
        above = centre(z + 1) if z + 1 < z_rows else value
        diffs = [d.astype(jnp.bfloat16) for d in (*differences(z, value), above - below)]
        inverse = lax.rsqrt(sum(d * d for d in diffs) + jnp.bfloat16(1))
        total = total + value
        passed_next = jnp.exp2(total * (-factor * LOG2E))
        grown_next = jnp.exp2(total * (factor * LOG2E))
        dense = value.astype(jnp.bfloat16)
        for view, step in enumerate((passed - passed_next, grown_next - grown)):
            facing = sum(d * light[z * 6 + view * 3 + k] for k, d in enumerate(diffs))
            shade = jnp.bfloat16(1) + jnp.abs(facing) * inverse
            weight = step.astype(jnp.bfloat16) * shade
            terms[view][0].append(weight)
            terms[view][1].append(dense * weight)
        if len(terms[0][0]) == depth:
            for view in range(2):
                rows = [jnp.concatenate(t, 0) for t in terms[view]]
                sums[view] = sums[view] + jnp.dot(
                    adder, jnp.concatenate(rows, 1), preferred_element_type=jnp.float32
                )
            terms = [([], []), ([], [])]
        passed, grown = passed_next, grown_next
        below, value = value, above
    plain_0, dense_0 = (sums[0][:, i * LANES : (i + 1) * LANES] * AMBIENT for i in range(2))
    plain_1, dense_1 = (
        sums[1][:, i * LANES : (i + 1) * LANES] * (passed * AMBIENT) for i in range(2)
    )
    return plain_0, dense_0, plain_1, dense_1, total * factor


def adder_of(rows, depth):
    row = lax.broadcasted_iota(jnp.int32, (rows, rows * depth), 0)
    column = lax.broadcasted_iota(jnp.int32, (rows, rows * depth), 1)
    return (column % rows == row).astype(jnp.float32).astype(jnp.bfloat16)


def spread_light(light_ref, table, z_rows):
    shape = table.shape[1:]
    targets = [
        jnp.full(shape, light_ref[i // 3, i % 3] * (1 / AMBIENT), jnp.float32) for i in range(6)
    ]

    def body(z, errors):
        left = []
        for i in range(6):
            wanted = targets[i] + errors[i]
            rounded = wanted.astype(jnp.bfloat16)
            table[z * 6 + i] = rounded
            left.append(wanted - rounded.astype(jnp.float32))
        return tuple(left)

    lax.fori_loop(0, z_rows, body, tuple(jnp.zeros(shape, jnp.float32) for _ in range(6)))


def write_pixels(out, c, start, sums):
    for channel, image in enumerate(sums):
        out[c, channel, pl.ds(start, image.shape[0]), :] = image.astype(jnp.bfloat16)


def y_difference(buf, c, z, rows, value, first, last):
    left = buf[c, z, rows, :]
    right = buf[c + 2, z, rows, :]
    following = pltpu.roll(jnp.where(first, right, value), LANES - 1, 1)
    preceding = pltpu.roll(jnp.where(last, left, value), 1, 1)
    return following - preceding


def planes_kernel(density, low, high, sems):
    x_rows = density.shape[1]
    copies = [
        pltpu.make_async_copy(density.at[:, x, :], target, sems.at[i])
        for i, (x, target) in enumerate(((0, low), (x_rows - 1, high)))
    ]
    for copy in copies:
        copy.start()
    for copy in copies:
        copy.wait()


def boundary_planes(density):
    z_rows, _, columns = density.shape
    plane = jax.ShapeDtypeStruct((z_rows, columns), jnp.float32)
    vmem = pl.BlockSpec(memory_space=pltpu.VMEM)
    return pl.pallas_call(
        planes_kernel,
        out_shape=(plane, plane),
        in_specs=[pl.BlockSpec(memory_space=pltpu.HBM)],
        out_specs=(vmem, vmem),
        scratch_shapes=[pltpu.SemaphoreType.DMA((2,))],
        compiler_params=pltpu.CompilerParams(vmem_limit_bytes=2 * MIB),
        name="planes",
    )(density)


def lane_edges(shape):
    lane = lax.broadcasted_iota(jnp.int32, shape, 1)
    return lane == 0, lane == LANES - 1


def inner_kernel(factor, density, light_hbm, out, field, light, sems, light_ref, small):
    z_rows, x_rows, columns = density.shape
    count = columns // LANES

    def fetch(c):
        lanes = pl.ds(pl.multiple_of(c * LANES, LANES), LANES)
        return pltpu.make_async_copy(density.at[:, :, lanes], field.at[c + 1], sems.at[c])

    scalars = pltpu.make_async_copy(light_hbm, light_ref, small)
    scalars.start()
    for c in range(count):
        fetch(c).start()
    scalars.wait()
    first, last = lane_edges((2 * GROUP, LANES))
    adder = adder_of(2 * GROUP, 16)
    spread_light(light_ref, light, z_rows)
    fetch(0).wait()
    field[0] = pltpu.roll(field[1], LANES - 1, 2)

    def step(c):
        for start in range(GROUP, x_rows - GROUP, 2 * GROUP):
            rows = pl.ds(start, 2 * GROUP)

            def centre(z, rows=rows):
                return field[c + 1, z, rows, :]

            def differences(z, value, start=start, rows=rows):
                diff_x = (
                    field[c + 1, z, pl.ds(start + 1, 2 * GROUP), :]
                    - field[c + 1, z, pl.ds(start - 1, 2 * GROUP), :]
                )
                return diff_x, y_difference(field, c, z, rows, value, first, last)

            write_pixels(out, c, start, march(centre, differences, z_rows, light, adder, factor))

    def body(i, carry):
        for k in range(UNROLL - 1):
            fetch(i * UNROLL + k + 1).wait()

        @pl.when((i + 1) * UNROLL < count)
        def _():
            fetch((i + 1) * UNROLL).wait()

        @pl.when((i + 1) * UNROLL == count)
        def _():
            field[count + 1] = pltpu.roll(field[count], 1, 2)

        for k in range(UNROLL):
            step(i * UNROLL + k)
        return carry

    lax.fori_loop(0, count // UNROLL, body, 0)


def march_inner(density, light_dir, factor):
    z_rows, x_rows, columns = density.shape
    count = columns // LANES
    hbm = pl.BlockSpec(memory_space=pltpu.HBM)
    vmem = pl.BlockSpec(memory_space=pltpu.VMEM)
    return pl.pallas_call(
        functools.partial(inner_kernel, factor),
        out_shape=(
            jax.ShapeDtypeStruct((count, CHANNELS, x_rows, LANES), jnp.bfloat16),
            pltpu.VMEM((count + 2, z_rows, x_rows, LANES), jnp.float32),
            pltpu.VMEM((6 * z_rows, 2 * GROUP, LANES), jnp.bfloat16),
        ),
        in_specs=[hbm, hbm],
        out_specs=(vmem, vmem, vmem),
        scratch_shapes=[
            pltpu.SemaphoreType.DMA((count,)),
            pltpu.SMEM((2, 3), jnp.float32),
            pltpu.SemaphoreType.DMA(()),
        ],
        compiler_params=pltpu.CompilerParams(vmem_limit_bytes=4 * MIB),
        name="march_inner",
    )(density, light_dir)


def outer_kernel(factor, tiles, field, low, high, light, tile_ref, _, out):
    count, z_rows, x_rows = field.shape[0] - 2, field.shape[1], field.shape[2]
    top = x_rows - GROUP
    first, last = lane_edges((2 * GROUP, LANES))
    adder = adder_of(2 * GROUP, 16)
    row = lax.broadcasted_iota(jnp.int32, (GROUP, LANES), 0)
    is_low, is_high = row == 0, row == GROUP - 1
    tile = jnp.full((GROUP, LANES), tile_ref[0], jnp.int32)
    own_low, own_high = tile == 0, tile == tiles - 1

    def step(c):
        lanes = pl.ds(pl.multiple_of(c * LANES, LANES), LANES)

        def both(block, z):
            return jnp.concatenate([field[block, z, :GROUP, :], field[block, z, top:, :]], 0)

        def centre(z):
            return both(c + 1, z)

        def differences(z, value):
            head, tail = value[:GROUP], value[GROUP:]
            before = jnp.where(own_low, head, low[z : z + 1, lanes])
            after = jnp.where(own_high, tail, high[z : z + 1, lanes])
            before = jnp.where(is_low, before, pltpu.roll(head, 1, 0))
            after = jnp.where(is_high, after, pltpu.roll(tail, GROUP - 1, 0))
            diff_x = jnp.concatenate(
                [
                    field[c + 1, z, 1 : GROUP + 1, :] - before,
                    after - field[c + 1, z, top - 1 : x_rows - 1, :],
                ],
                0,
            )
            following = pltpu.roll(jnp.where(first, both(c + 2, z), value), LANES - 1, 1)
            preceding = pltpu.roll(jnp.where(last, both(c, z), value), 1, 1)
            return diff_x, following - preceding

        sums = march(centre, differences, z_rows, light, adder, factor)
        write_pixels(out, c, 0, [s[:GROUP] for s in sums])
        write_pixels(out, c, top, [s[GROUP:] for s in sums])

    def body(i, carry):
        for k in range(OUTER):
            step(i * OUTER + k)
        return carry

    lax.fori_loop(0, count // OUTER, body, 0)


def march_outer(field, low, high, light, tile, tiles, colours, factor):
    smem = pl.BlockSpec(memory_space=pltpu.SMEM)
    vmem = pl.BlockSpec(memory_space=pltpu.VMEM)
    return pl.pallas_call(
        functools.partial(outer_kernel, factor, tiles),
        out_shape=jax.ShapeDtypeStruct(colours.shape, jnp.bfloat16),
        in_specs=[vmem, vmem, vmem, vmem, smem, vmem],
        out_specs=vmem,
        input_output_aliases={5: 0},
        compiler_params=pltpu.CompilerParams(vmem_limit_bytes=4 * MIB),
        name="march_outer",
    )(field, low, high, light, tile, colours)


def compose_kernel(slab_ref, palette_ref, source, out, order):
    slabs = source.shape[0]
    for b in range(slabs):
        order[slab_ref[b]] = b
    shape = source.shape[2:]
    for view in range(2):
        front = plain = dense = jnp.zeros(shape, jnp.float32)
        for position in range(slabs) if view == 0 else reversed(range(slabs)):
            b = order[position]
            fading = jnp.exp(-front)
            plain = plain + source[b, view * 2].astype(jnp.float32) * fading
            dense = dense + source[b, view * 2 + 1].astype(jnp.float32) * fading
            front = front + source[b, 4].astype(jnp.float32)
        for k in range(3):
            out[view, k] = palette_ref[0, k] * plain + palette_ref[1, k] * dense
        if view == 0:
            out[0, 3] = out[1, 3] = 1.0 - jnp.exp(-front)


def compose(slab_of, palette, source):
    smem = pl.BlockSpec(memory_space=pltpu.SMEM)
    vmem = pl.BlockSpec(memory_space=pltpu.VMEM)
    return pl.pallas_call(
        compose_kernel,
        out_shape=jax.ShapeDtypeStruct((2, 4, *source.shape[2:]), jnp.float32),
        in_specs=[smem, smem, vmem],
        out_specs=vmem,
        scratch_shapes=[pltpu.SMEM((slab_of.shape[0],), jnp.int32)],
        compiler_params=pltpu.CompilerParams(vmem_limit_bytes=4 * MIB),
        name="compose",
    )(slab_of, palette, source)


def on_device(density, palette, light_dir, slab_of):
    factor = 3.0 / (density.shape[0] * lax.axis_size("depth"))
    tiles = lax.axis_size("tile")
    forward = [(i, i + 1) for i in range(tiles - 1)]
    backward = [(i + 1, i) for i in range(tiles - 1)]
    density, light_dir = (
        pltpu.with_memory_space_constraint(a, pltpu.HBM) for a in (density, light_dir)
    )
    low, high = boundary_planes(density)
    from_low = lax.ppermute(high, "tile", forward)
    from_high = lax.ppermute(low, "tile", backward)
    colours, field, light = march_inner(density, light_dir, factor)
    tile = lax.axis_index("tile")[None]
    colours = march_outer(field, from_low, from_high, light, tile, tiles, colours, factor)
    return compose(slab_of, palette, lax.all_to_all(colours, "depth", 0, 0, tiled=True))


def solution(mesh):
    in_specs = (P("depth", "tile", None), P(), P(), P())
    out_specs = P(None, None, "tile", "depth")
    return jax.shard_map(
        on_device, mesh=mesh, in_specs=in_specs, out_specs=out_specs, check_vma=False
    )
```

```python
import functools
import math

import jax
import jax.numpy as jnp
from jax import lax
from jax.experimental import pallas as pl
from jax.experimental.pallas import tpu as pltpu
from jax.sharding import PartitionSpec as P

LANES = 128
GROUP = 8
CHANNELS = 5
AMBIENT = 0.3
MIB = 2**20
UNROLL = 4
OUTER = 16
LOG2E = math.log2(math.e)


def march(centre, differences, z_rows, light, adder, factor):
    value = centre(0)
    below = value
    total = jnp.zeros(value.shape, jnp.float32)
    passed = grown = jnp.ones(value.shape, jnp.float32)
    depth = adder.shape[1] // value.shape[0]
    sums = [jnp.zeros((value.shape[0], 2 * LANES), jnp.float32) for _ in range(2)]
    terms = [([], []), ([], [])]
    for z in range(z_rows):
        above = centre(z + 1) if z + 1 < z_rows else value
        diffs = [d.astype(jnp.bfloat16) for d in (*differences(z, value), above - below)]
        inverse = lax.rsqrt(sum(d * d for d in diffs) + jnp.bfloat16(1))
        total = total + value
        passed_next = jnp.exp2(total * (-factor * LOG2E))
        grown_next = jnp.exp2(total * (factor * LOG2E))
        dense = value.astype(jnp.bfloat16)
        for view, step in enumerate((passed - passed_next, grown_next - grown)):
            facing = sum(d * light[z * 6 + view * 3 + k] for k, d in enumerate(diffs))
            shade = jnp.bfloat16(1) + jnp.abs(facing) * inverse
            weight = step.astype(jnp.bfloat16) * shade
            terms[view][0].append(weight)
            terms[view][1].append(dense * weight)
        if len(terms[0][0]) == depth:
            for view in range(2):
                rows = [jnp.concatenate(t, 0) for t in terms[view]]
                sums[view] = sums[view] + jnp.dot(
                    adder, jnp.concatenate(rows, 1), preferred_element_type=jnp.float32
                )
            terms = [([], []), ([], [])]
        passed, grown = passed_next, grown_next
        below, value = value, above
    plain_0, dense_0 = (sums[0][:, i * LANES : (i + 1) * LANES] * AMBIENT for i in range(2))
    plain_1, dense_1 = (
        sums[1][:, i * LANES : (i + 1) * LANES] * (passed * AMBIENT) for i in range(2)
    )
    return plain_0, dense_0, plain_1, dense_1, total * factor


def adder_of(rows, depth):
    row = lax.broadcasted_iota(jnp.int32, (rows, rows * depth), 0)
    column = lax.broadcasted_iota(jnp.int32, (rows, rows * depth), 1)
    return (column % rows == row).astype(jnp.float32).astype(jnp.bfloat16)


def spread_light(light_ref, table, z_rows):
    shape = table.shape[1:]
    targets = [
        jnp.full(shape, light_ref[i // 3, i % 3] * (1 / AMBIENT), jnp.float32) for i in range(6)
    ]

    def body(z, errors):
        left = []
        for i in range(6):
            wanted = targets[i] + errors[i]
            rounded = wanted.astype(jnp.bfloat16)
            table[z * 6 + i] = rounded
            left.append(wanted - rounded.astype(jnp.float32))
        return tuple(left)

    lax.fori_loop(0, z_rows, body, tuple(jnp.zeros(shape, jnp.float32) for _ in range(6)))


def write_pixels(out, c, start, sums):
    for channel, image in enumerate(sums):
        out[c, channel, pl.ds(start, image.shape[0]), :] = image.astype(jnp.bfloat16)


def y_difference(buf, c, z, rows, value, first, last):
    left = buf[c, z, rows, :]
    right = buf[c + 2, z, rows, :]
    following = pltpu.roll(jnp.where(first, right, value), LANES - 1, 1)
    preceding = pltpu.roll(jnp.where(last, left, value), 1, 1)
    return following - preceding


def planes_kernel(density, near, far, sems):
    top = density.shape[1] - 1
    side = (lax.axis_index("tile") % 2) * top
    copies = [
        pltpu.make_async_copy(density.at[:, x, :], target, sems.at[i])
        for i, (x, target) in enumerate(((top - side, near), (side, far)))
    ]
    for copy in copies:
        copy.start()
    for copy in copies:
        copy.wait()


def boundary_planes(density):
    z_rows, _, columns = density.shape
    plane = jax.ShapeDtypeStruct((z_rows, columns), jnp.float32)
    vmem = pl.BlockSpec(memory_space=pltpu.VMEM)
    return pl.pallas_call(
        planes_kernel,
        out_shape=(plane, plane),
        in_specs=[pl.BlockSpec(memory_space=pltpu.HBM)],
        out_specs=(vmem, vmem),
        scratch_shapes=[pltpu.SemaphoreType.DMA((2,))],
        compiler_params=pltpu.CompilerParams(vmem_limit_bytes=2 * MIB),
        name="planes",
    )(density)


def lane_edges(shape):
    lane = lax.broadcasted_iota(jnp.int32, shape, 1)
    return lane == 0, lane == LANES - 1


def inner_kernel(factor, density, light_hbm, out, field, light, sems, light_ref, small):
    z_rows, x_rows, columns = density.shape
    count = columns // LANES

    def fetch(c):
        lanes = pl.ds(pl.multiple_of(c * LANES, LANES), LANES)
        return pltpu.make_async_copy(density.at[:, :, lanes], field.at[c + 1], sems.at[c])

    scalars = pltpu.make_async_copy(light_hbm, light_ref, small)
    scalars.start()
    for c in range(count):
        fetch(c).start()
    scalars.wait()
    first, last = lane_edges((2 * GROUP, LANES))
    adder = adder_of(2 * GROUP, 16)
    spread_light(light_ref, light, z_rows)
    fetch(0).wait()
    field[0] = pltpu.roll(field[1], LANES - 1, 2)

    def step(c):
        for start in range(GROUP, x_rows - GROUP, 2 * GROUP):
            rows = pl.ds(start, 2 * GROUP)

            def centre(z, rows=rows):
                return field[c + 1, z, rows, :]

            def differences(z, value, start=start, rows=rows):
                diff_x = (
                    field[c + 1, z, pl.ds(start + 1, 2 * GROUP), :]
                    - field[c + 1, z, pl.ds(start - 1, 2 * GROUP), :]
                )
                return diff_x, y_difference(field, c, z, rows, value, first, last)

            write_pixels(out, c, start, march(centre, differences, z_rows, light, adder, factor))

    def group(start, size):
        for k in range(1, size):
            fetch(start + k).wait()

        @pl.when(start + size < count)
        def _():
            fetch(start + size).wait()

        @pl.when(start + size == count)
        def _():
            field[count + 1] = pltpu.roll(field[count], 1, 2)

        for k in range(size):
            step(start + k)

    def body(i, carry):
        group(i * UNROLL, UNROLL)
        return carry

    group(0, 1)
    group(1, UNROLL - 1)
    lax.fori_loop(1, count // UNROLL, body, 0)


def march_inner(density, light_dir, factor):
    z_rows, x_rows, columns = density.shape
    count = columns // LANES
    hbm = pl.BlockSpec(memory_space=pltpu.HBM)
    vmem = pl.BlockSpec(memory_space=pltpu.VMEM)
    return pl.pallas_call(
        functools.partial(inner_kernel, factor),
        out_shape=(
            jax.ShapeDtypeStruct((count, CHANNELS, x_rows, LANES), jnp.bfloat16),
            pltpu.VMEM((count + 2, z_rows, x_rows, LANES), jnp.float32),
            pltpu.VMEM((6 * z_rows, 2 * GROUP, LANES), jnp.bfloat16),
        ),
        in_specs=[hbm, hbm],
        out_specs=(vmem, vmem, vmem),
        scratch_shapes=[
            pltpu.SemaphoreType.DMA((count,)),
            pltpu.SMEM((2, 3), jnp.float32),
            pltpu.SemaphoreType.DMA(()),
        ],
        compiler_params=pltpu.CompilerParams(vmem_limit_bytes=4 * MIB),
        name="march_inner",
    )(density, light_dir)


def outer_kernel(factor, tiles, field, near, far, light, _, out, halo):
    count, z_rows, x_rows = field.shape[0] - 2, field.shape[1], field.shape[2]
    top = x_rows - GROUP
    first, last = lane_edges((2 * GROUP, LANES))
    adder = adder_of(2 * GROUP, 16)
    row = lax.broadcasted_iota(jnp.int32, (GROUP, LANES), 0)
    is_low, is_high = row == 0, row == GROUP - 1
    place = lax.axis_index("tile")
    odd = place % 2
    halo[1 - odd] = near[...]
    halo[odd] = far[...]
    tile = jnp.full((GROUP, LANES), place, jnp.int32)
    own_low, own_high = tile == 0, tile == tiles - 1

    def step(c):
        lanes = pl.ds(pl.multiple_of(c * LANES, LANES), LANES)

        def both(block, z):
            return jnp.concatenate([field[block, z, :GROUP, :], field[block, z, top:, :]], 0)

        def centre(z):
            return both(c + 1, z)

        def differences(z, value):
            head, tail = value[:GROUP], value[GROUP:]
            before = jnp.where(own_low, head, halo[0, z : z + 1, lanes])
            after = jnp.where(own_high, tail, halo[1, z : z + 1, lanes])
            before = jnp.where(is_low, before, pltpu.roll(head, 1, 0))
            after = jnp.where(is_high, after, pltpu.roll(tail, GROUP - 1, 0))
            diff_x = jnp.concatenate(
                [
                    field[c + 1, z, 1 : GROUP + 1, :] - before,
                    after - field[c + 1, z, top - 1 : x_rows - 1, :],
                ],
                0,
            )
            following = pltpu.roll(jnp.where(first, both(c + 2, z), value), LANES - 1, 1)
            preceding = pltpu.roll(jnp.where(last, both(c, z), value), 1, 1)
            return diff_x, following - preceding

        sums = march(centre, differences, z_rows, light, adder, factor)
        write_pixels(out, c, 0, [s[:GROUP] for s in sums])
        write_pixels(out, c, top, [s[GROUP:] for s in sums])

    def body(i, carry):
        for k in range(OUTER):
            step(i * OUTER + k)
        return carry

    lax.fori_loop(0, count // OUTER, body, 0)


def march_outer(field, near, far, light, tiles, colours, factor):
    vmem = pl.BlockSpec(memory_space=pltpu.VMEM)
    return pl.pallas_call(
        functools.partial(outer_kernel, factor, tiles),
        out_shape=jax.ShapeDtypeStruct(colours.shape, jnp.bfloat16),
        in_specs=[vmem, vmem, vmem, vmem, vmem],
        out_specs=vmem,
        scratch_shapes=[pltpu.VMEM((2, *near.shape), jnp.float32)],
        input_output_aliases={4: 0},
        compiler_params=pltpu.CompilerParams(vmem_limit_bytes=4 * MIB),
        name="march_outer",
    )(field, near, far, light, colours)


def compose_kernel(slab_ref, palette_ref, source, out, order):
    slabs = source.shape[0]
    for b in range(slabs):
        order[slab_ref[b]] = b
    shape = source.shape[2:]
    for view in range(2):
        front = plain = dense = jnp.zeros(shape, jnp.float32)
        for position in range(slabs) if view == 0 else reversed(range(slabs)):
            b = order[position]
            fading = jnp.exp(-front)
            plain = plain + source[b, view * 2].astype(jnp.float32) * fading
            dense = dense + source[b, view * 2 + 1].astype(jnp.float32) * fading
            front = front + source[b, 4].astype(jnp.float32)
        for k in range(3):
            out[view, k] = palette_ref[0, k] * plain + palette_ref[1, k] * dense
        if view == 0:
            out[0, 3] = out[1, 3] = 1.0 - jnp.exp(-front)


def compose(slab_of, palette, source):
    smem = pl.BlockSpec(memory_space=pltpu.SMEM)
    vmem = pl.BlockSpec(memory_space=pltpu.VMEM)
    return pl.pallas_call(
        compose_kernel,
        out_shape=jax.ShapeDtypeStruct((2, 4, *source.shape[2:]), jnp.float32),
        in_specs=[smem, smem, vmem],
        out_specs=vmem,
        scratch_shapes=[pltpu.SMEM((slab_of.shape[0],), jnp.int32)],
        compiler_params=pltpu.CompilerParams(vmem_limit_bytes=4 * MIB),
        name="compose",
    )(slab_of, palette, source)


def on_device(density, palette, light_dir, slab_of):
    factor = 3.0 / (density.shape[0] * lax.axis_size("depth"))
    tiles = lax.axis_size("tile")
    beside = [(i, i ^ 1) for i in range(tiles)]
    across = [(i, i + 1) for i in range(1, tiles - 1, 2)]
    across = across + [(j, i) for i, j in across]
    density, light_dir = (
        pltpu.with_memory_space_constraint(a, pltpu.HBM) for a in (density, light_dir)
    )
    near, far = boundary_planes(density)
    near = lax.ppermute(near, "tile", beside)
    far = lax.ppermute(far, "tile", across)
    colours, field, light = march_inner(density, light_dir, factor)
    colours = march_outer(field, near, far, light, tiles, colours, factor)
    return compose(slab_of, palette, lax.all_to_all(colours, "depth", 0, 0, tiled=True))


def solution(mesh):
    in_specs = (P("depth", "tile", None), P(), P(), P())
    out_specs = P(None, None, "tile", "depth")
    return jax.shard_map(
        on_device, mesh=mesh, in_specs=in_specs, out_specs=out_specs, check_vma=False
    )
```

```python
import functools
import math

import jax
import jax.numpy as jnp
from jax import lax
from jax.experimental import pallas as pl
from jax.experimental.pallas import tpu as pltpu
from jax.sharding import PartitionSpec as P

LANES = 128
GROUP = 8
CHANNELS = 5
AMBIENT = 0.3
MIB = 2**20
UNROLL = 4
OUTER = 16
LOG2E = math.log2(math.e)


def march(centre, differences, z_rows, light, adder, factor):
    value = centre(0)
    below = value
    total = jnp.zeros(value.shape, jnp.float32)
    passed = grown = jnp.ones(value.shape, jnp.float32)
    depth = adder.shape[1] // value.shape[0]
    sums = [jnp.zeros((value.shape[0], 2 * LANES), jnp.float32) for _ in range(2)]
    terms = [([], []), ([], [])]
    for z in range(z_rows):
        above = centre(z + 1) if z + 1 < z_rows else value
        diffs = [d.astype(jnp.bfloat16) for d in (*differences(z, value), above - below)]
        dx, dy, dz = diffs
        inverse = lax.rsqrt((dx * dx + jnp.bfloat16(1)) + (dy * dy + dz * dz))
        total = total + value
        passed_next = jnp.exp2(total * (-factor * LOG2E))
        grown_next = jnp.exp2(total * (factor * LOG2E))
        dense = value.astype(jnp.bfloat16)
        for view, step in enumerate((passed - passed_next, grown_next - grown)):
            lx, ly, lz = (light[z * 6 + view * 3 + k] for k in range(3))
            facing = dx * lx + dy * ly + dz * lz
            shade = jnp.bfloat16(1) + jnp.abs(facing) * inverse
            weight = step.astype(jnp.bfloat16) * shade
            terms[view][0].append(weight)
            terms[view][1].append(dense * weight)
        if len(terms[0][0]) == depth:
            for view in range(2):
                rows = [jnp.concatenate(t, 0) for t in terms[view]]
                sums[view] = sums[view] + jnp.dot(
                    adder, jnp.concatenate(rows, 1), preferred_element_type=jnp.float32
                )
            terms = [([], []), ([], [])]
        passed, grown = passed_next, grown_next
        below, value = value, above
    plain_0, dense_0 = (sums[0][:, i * LANES : (i + 1) * LANES] * AMBIENT for i in range(2))
    plain_1, dense_1 = (
        sums[1][:, i * LANES : (i + 1) * LANES] * (passed * AMBIENT) for i in range(2)
    )
    return plain_0, dense_0, plain_1, dense_1, total * factor


def adder_of(rows, depth):
    row = lax.broadcasted_iota(jnp.int32, (rows, rows * depth), 0)
    column = lax.broadcasted_iota(jnp.int32, (rows, rows * depth), 1)
    return (column % rows == row).astype(jnp.float32).astype(jnp.bfloat16)


def spread_light(light_ref, table, z_rows):
    shape = table.shape[1:]
    targets = [
        jnp.full(shape, light_ref[i // 3, i % 3] * (1 / AMBIENT), jnp.float32) for i in range(6)
    ]

    def body(z, errors):
        left = []
        for i in range(6):
            wanted = targets[i] + errors[i]
            rounded = wanted.astype(jnp.bfloat16)
            table[z * 6 + i] = rounded
            left.append(wanted - rounded.astype(jnp.float32))
        return tuple(left)

    lax.fori_loop(0, z_rows, body, tuple(jnp.zeros(shape, jnp.float32) for _ in range(6)))


def write_pixels(out, c, start, sums):
    for channel, image in enumerate(sums):
        out[c, channel, pl.ds(start, image.shape[0]), :] = image.astype(jnp.bfloat16)


def y_difference(buf, c, z, rows, value, first, last):
    left = buf[c, z, rows, :]
    right = buf[c + 2, z, rows, :]
    following = pltpu.roll(jnp.where(first, right, value), LANES - 1, 1)
    preceding = pltpu.roll(jnp.where(last, left, value), 1, 1)
    return following - preceding


def planes_kernel(density, near, far, sems):
    top = density.shape[1] - 1
    side = (lax.axis_index("tile") % 2) * top
    copies = [
        pltpu.make_async_copy(density.at[:, x, :], target, sems.at[i])
        for i, (x, target) in enumerate(((top - side, near), (side, far)))
    ]
    for copy in copies:
        copy.start()
    for copy in copies:
        copy.wait()


def boundary_planes(density):
    z_rows, _, columns = density.shape
    plane = jax.ShapeDtypeStruct((z_rows, columns), jnp.float32)
    vmem = pl.BlockSpec(memory_space=pltpu.VMEM)
    return pl.pallas_call(
        planes_kernel,
        out_shape=(plane, plane),
        in_specs=[pl.BlockSpec(memory_space=pltpu.HBM)],
        out_specs=(vmem, vmem),
        scratch_shapes=[pltpu.SemaphoreType.DMA((2,))],
        compiler_params=pltpu.CompilerParams(vmem_limit_bytes=2 * MIB),
        name="planes",
    )(density)


def lane_edges(shape):
    lane = lax.broadcasted_iota(jnp.int32, shape, 1)
    return lane == 0, lane == LANES - 1


def inner_kernel(factor, density, light_hbm, out, field, light, sems, light_ref, small):
    z_rows, x_rows, columns = density.shape
    count = columns // LANES

    def fetch(c):
        lanes = pl.ds(pl.multiple_of(c * LANES, LANES), LANES)
        return pltpu.make_async_copy(density.at[:, :, lanes], field.at[c + 1], sems.at[c])

    scalars = pltpu.make_async_copy(light_hbm, light_ref, small)
    scalars.start()
    for c in range(count):
        fetch(c).start()
    scalars.wait()
    first, last = lane_edges((2 * GROUP, LANES))
    adder = adder_of(2 * GROUP, 16)
    spread_light(light_ref, light, z_rows)
    fetch(0).wait()
    field[0] = pltpu.roll(field[1], LANES - 1, 2)

    def step(c):
        for start in range(GROUP, x_rows - GROUP, 2 * GROUP):
            rows = pl.ds(start, 2 * GROUP)

            def centre(z, rows=rows):
                return field[c + 1, z, rows, :]

            def differences(z, value, start=start, rows=rows):
                diff_x = (
                    field[c + 1, z, pl.ds(start + 1, 2 * GROUP), :]
                    - field[c + 1, z, pl.ds(start - 1, 2 * GROUP), :]
                )
                return diff_x, y_difference(field, c, z, rows, value, first, last)

            write_pixels(out, c, start, march(centre, differences, z_rows, light, adder, factor))

    def group(start, size):
        for k in range(1, size):
            fetch(start + k).wait()

        @pl.when(start + size < count)
        def _():
            fetch(start + size).wait()

        @pl.when(start + size == count)
        def _():
            field[count + 1] = pltpu.roll(field[count], 1, 2)

        for k in range(size):
            step(start + k)

    def body(i, carry):
        group(i * UNROLL, UNROLL)
        return carry

    group(0, 1)
    group(1, UNROLL - 1)
    lax.fori_loop(1, count // UNROLL, body, 0)


def march_inner(density, light_dir, factor):
    z_rows, x_rows, columns = density.shape
    count = columns // LANES
    hbm = pl.BlockSpec(memory_space=pltpu.HBM)
    vmem = pl.BlockSpec(memory_space=pltpu.VMEM)
    return pl.pallas_call(
        functools.partial(inner_kernel, factor),
        out_shape=(
            jax.ShapeDtypeStruct((count, CHANNELS, x_rows, LANES), jnp.bfloat16),
            pltpu.VMEM((count + 2, z_rows, x_rows, LANES), jnp.float32),
            pltpu.VMEM((6 * z_rows, 2 * GROUP, LANES), jnp.bfloat16),
        ),
        in_specs=[hbm, hbm],
        out_specs=(vmem, vmem, vmem),
        scratch_shapes=[
            pltpu.SemaphoreType.DMA((count,)),
            pltpu.SMEM((2, 3), jnp.float32),
            pltpu.SemaphoreType.DMA(()),
        ],
        compiler_params=pltpu.CompilerParams(vmem_limit_bytes=4 * MIB),
        name="march_inner",
    )(density, light_dir)


def outer_kernel(factor, tiles, field, near, far, light, _, out, halo):
    count, z_rows, x_rows = field.shape[0] - 2, field.shape[1], field.shape[2]
    top = x_rows - GROUP
    first, last = lane_edges((2 * GROUP, LANES))
    adder = adder_of(2 * GROUP, 16)
    row = lax.broadcasted_iota(jnp.int32, (GROUP, LANES), 0)
    is_low, is_high = row == 0, row == GROUP - 1
    place = lax.axis_index("tile")
    odd = place % 2
    halo[1 - odd] = near[...]
    halo[odd] = far[...]
    tile = jnp.full((GROUP, LANES), place, jnp.int32)
    own_low, own_high = tile == 0, tile == tiles - 1

    def step(c):
        lanes = pl.ds(pl.multiple_of(c * LANES, LANES), LANES)

        def both(block, z):
            return jnp.concatenate([field[block, z, :GROUP, :], field[block, z, top:, :]], 0)

        def centre(z):
            return both(c + 1, z)

        def differences(z, value):
            head, tail = value[:GROUP], value[GROUP:]
            before = jnp.where(own_low, head, halo[0, z : z + 1, lanes])
            after = jnp.where(own_high, tail, halo[1, z : z + 1, lanes])
            before = jnp.where(is_low, before, pltpu.roll(head, 1, 0))
            after = jnp.where(is_high, after, pltpu.roll(tail, GROUP - 1, 0))
            diff_x = jnp.concatenate(
                [
                    field[c + 1, z, 1 : GROUP + 1, :] - before,
                    after - field[c + 1, z, top - 1 : x_rows - 1, :],
                ],
                0,
            )
            following = pltpu.roll(jnp.where(first, both(c + 2, z), value), LANES - 1, 1)
            preceding = pltpu.roll(jnp.where(last, both(c, z), value), 1, 1)
            return diff_x, following - preceding

        sums = march(centre, differences, z_rows, light, adder, factor)
        write_pixels(out, c, 0, [s[:GROUP] for s in sums])
        write_pixels(out, c, top, [s[GROUP:] for s in sums])

    def body(i, carry):
        for k in range(OUTER):
            step(i * OUTER + k)
        return carry

    lax.fori_loop(0, count // OUTER, body, 0)


def march_outer(field, near, far, light, tiles, colours, factor):
    vmem = pl.BlockSpec(memory_space=pltpu.VMEM)
    return pl.pallas_call(
        functools.partial(outer_kernel, factor, tiles),
        out_shape=jax.ShapeDtypeStruct(colours.shape, jnp.bfloat16),
        in_specs=[vmem, vmem, vmem, vmem, vmem],
        out_specs=vmem,
        scratch_shapes=[pltpu.VMEM((2, *near.shape), jnp.float32)],
        input_output_aliases={4: 0},
        compiler_params=pltpu.CompilerParams(vmem_limit_bytes=4 * MIB),
        name="march_outer",
    )(field, near, far, light, colours)


def compose_kernel(slab_ref, palette_ref, source, out, order):
    slabs = source.shape[0]
    for b in range(slabs):
        order[slab_ref[b]] = b
    shape = source.shape[2:]
    for view in range(2):
        front = plain = dense = jnp.zeros(shape, jnp.float32)
        for position in range(slabs) if view == 0 else reversed(range(slabs)):
            b = order[position]
            fading = jnp.exp(-front)
            plain = plain + source[b, view * 2].astype(jnp.float32) * fading
            dense = dense + source[b, view * 2 + 1].astype(jnp.float32) * fading
            front = front + source[b, 4].astype(jnp.float32)
        for k in range(3):
            out[view, k] = palette_ref[0, k] * plain + palette_ref[1, k] * dense
        if view == 0:
            out[0, 3] = out[1, 3] = 1.0 - jnp.exp(-front)


def compose(slab_of, palette, source):
    smem = pl.BlockSpec(memory_space=pltpu.SMEM)
    vmem = pl.BlockSpec(memory_space=pltpu.VMEM)
    return pl.pallas_call(
        compose_kernel,
        out_shape=jax.ShapeDtypeStruct((2, 4, *source.shape[2:]), jnp.float32),
        in_specs=[smem, smem, vmem],
        out_specs=vmem,
        scratch_shapes=[pltpu.SMEM((slab_of.shape[0],), jnp.int32)],
        compiler_params=pltpu.CompilerParams(vmem_limit_bytes=4 * MIB),
        name="compose",
    )(slab_of, palette, source)


def on_device(density, palette, light_dir, slab_of):
    factor = 3.0 / (density.shape[0] * lax.axis_size("depth"))
    tiles = lax.axis_size("tile")
    beside = [(i, i ^ 1) for i in range(tiles)]
    across = [(i, i + 1) for i in range(1, tiles - 1, 2)]
    across = across + [(j, i) for i, j in across]
    density, light_dir = (
        pltpu.with_memory_space_constraint(a, pltpu.HBM) for a in (density, light_dir)
    )
    near, far = boundary_planes(density)
    near = lax.ppermute(near, "tile", beside)
    far = lax.ppermute(far, "tile", across)
    colours, field, light = march_inner(density, light_dir, factor)
    colours = march_outer(field, near, far, light, tiles, colours, factor)
    return compose(slab_of, palette, lax.all_to_all(colours, "depth", 0, 0, tiled=True))


def solution(mesh):
    in_specs = (P("depth", "tile", None), P(), P(), P())
    out_specs = P(None, None, "tile", "depth")
    return jax.shard_map(
        on_device, mesh=mesh, in_specs=in_specs, out_specs=out_specs, check_vma=False
    )
```
